32 devices in a mesh: row: 4 (over x, core), col: 8 (over z, y).
Axes of the slice: x: 2, y: 2, z: 4, core: 2. Of those that a mesh axis runs over, the one named last changes fastest.
Arguments:
- gate_act: bfloat16 [256, 14336], P(('row', 'col')), may hold values from -6 to 6
- up_act: bfloat16 [256, 14336], P(('row', 'col')), may hold values from -6 to 6
- running_hessian: float32 [14336, 14336], P('row', 'col'), may hold values from -0.03 to 2.02, as said below
Outputs:
- new_hessian: float32 [14336, 14336], P('row', 'col')
The draws below stay inside these ranges and needn't reach their ends.
Inputs may be any that keep to these rules, and one draw needn't show every extreme that they name: `running_hessian`: symmetric.
All inputs are finite; a program needn't handle non-finite values.
Results may differ from the reference program's by a relative error of at most 0.0026.
Values may be sent and summed in bfloat16 or wider, within the bound.
A program may use at most 128 MiB of HBM per device.

```python
import jax
import jax.numpy as jnp

FEAT = 14336
TOKENS = 256
PRIOR = 768


def draw_running_hessian(key, part):
    first, second = jax.random.split(key)
    noise = jnp.clip(jax.random.normal(first, (FEAT, FEAT), jnp.float32), -4.0, 4.0) * 0.002
    diag_vals = jnp.exp(jax.random.uniform(second, (FEAT,), jnp.float32, jnp.log(0.2), jnp.log(2.0)))
    return noise + noise.T + jnp.diag(diag_vals)


def block_levels(own_key, dims, shards, smallest, high):
    factor_of, own = 1.0, jax.random.fold_in(own_key, 6)
    for position, parts in shards:
        draws = jnp.exp(jax.random.uniform(jax.random.fold_in(own, position), (parts,), jnp.float32, smallest / len(shards), high / len(shards)))
        factor_of = factor_of * jnp.repeat(draws, dims[position] // parts).reshape([-1 if axis == position else 1 for axis in range(len(dims))])
    return factor_of


def normal_values(own_key, extent, scale, reach, pieces=(), kind=jnp.bfloat16):
    loudness = block_levels(own_key, extent, pieces, -0.22, 0.18) if pieces else 1.0
    result = jax.random.normal(own_key, extent, jnp.float32) * scale * loudness
    return jnp.minimum(jnp.maximum(result, -reach), reach).astype(kind)


def setup_inputs(seed: int = 0) -> dict:
    splits = jax.random.split(jax.random.key(seed), 4)
    gate_act = normal_values(splits[0], (TOKENS, FEAT), 1.0, 6.0, ((0, 32),))
    up_act = normal_values(splits[1], (TOKENS, FEAT), 1.0, 6.0, ((0, 32),))
    running_hessian = draw_running_hessian(jax.random.fold_in(splits[3], 71), 0)
    return {"gate_act": gate_act, "up_act": up_act, "running_hessian": running_hessian}


def reference(gate_act, up_act, running_hessian):
    inputs = (jax.nn.silu(gate_act.astype(jnp.float32)) * up_act.astype(jnp.float32)).astype(jnp.bfloat16)
    gram = jnp.dot(inputs.T, inputs, preferred_element_type=jnp.float32)
    total = PRIOR + TOKENS
    return (PRIOR / total) * running_hessian + (2.0 / total) * gram
```

```python
import functools

import jax
import jax.numpy as jnp
from jax import lax
from jax.experimental import pallas as pl
from jax.experimental.pallas import tpu as pltpu
from jax.sharding import PartitionSpec as P

MESH = pl.DeviceIdType.MESH
LANES = 128
HESS_PARTS = 8
LAG = 2


def plain_inputs(gate_act, up_act):
    return (jax.nn.silu(gate_act.astype(jnp.float32)) * up_act.astype(jnp.float32)).astype(
        jnp.bfloat16
    )


def on_device_plain(gate_act, up_act, running_hessian):
    n_row = lax.axis_size("row")
    n_col = lax.axis_size("col")
    tok_dev = gate_act.shape[0]
    col_width = running_hessian.shape[1]
    inputs = plain_inputs(gate_act, up_act)
    col_part = lax.all_to_all(inputs, "col", split_axis=1, concat_axis=0, tiled=True)
    col_panel = lax.all_gather(col_part, "row", axis=0, tiled=True)
    col_ordered = (
        col_panel.reshape(n_row, n_col, tok_dev, col_width).swapaxes(0, 1).reshape(-1, col_width)
    )
    row_part = lax.all_to_all(inputs, "row", split_axis=1, concat_axis=0, tiled=True)
    gram = lax.dot_general(
        lax.all_gather(row_part, "col", axis=0, tiled=True),
        col_ordered,
        (((0,), (0,)), ((), ())),
        preferred_element_type=jnp.float32,
    )
    tokens_all = tok_dev * n_row * n_col
    total = 4.0 * tokens_all
    return 3.0 * tokens_all / total * running_hessian + 2.0 / total * gram


def other_core(r):
    return r + 1 - 2 * lax.rem(r, 2)


def gather_kernel(
    n_row, n_col, gate_ref, up_ref, hess_hbm, row_ref, col_ref, hess_ref, own,
    hess_sem, own_sem, x_send, x_recv, ring_send, ring_recv, c_send, c_recv, c_local,
):
    tok, width = gate_ref.shape[0], row_ref.shape[1]
    half_width = col_ref.shape[1]
    r, c = lax.axis_index("row"), lax.axis_index("col")
    sib = other_core(r)
    far = lax.rem(r + 2, n_row)
    far_sib = other_core(far)
    peers = (sib, far, far_sib)

    y = lax.rem(c, 2)
    place = (1 - y) * lax.div(c, 2) + y * (n_col - 1 - lax.div(c, 2))

    def at(p):
        p = lax.rem(p + 2 * n_col, n_col)
        back = lax.div(p, n_col // 2)
        return (1 - back) * 2 * p + back * (2 * (n_col - 1 - p) + 1)

    nexts = (at(place + 1), at(place - 1))

    hess_rows = hess_ref.shape[0] // HESS_PARTS
    hess_copies = []
    for i in range(HESS_PARTS):
        part = pl.ds(i * hess_rows, hess_rows)
        hess_copies.append(
            pltpu.make_async_copy(hess_hbm.at[part], hess_ref.at[part], hess_sem.at[i])
        )

    barrier = pltpu.get_barrier_semaphore()
    for peer in peers:
        pl.semaphore_signal(barrier, inc=1, device_id={"row": peer, "col": c}, device_id_type=MESH)
    for peer in nexts:
        pl.semaphore_signal(barrier, inc=1, device_id={"row": r, "col": peer}, device_id_type=MESH)

    gate = gate_ref[...].astype(jnp.float32)
    own[...] = (jax.nn.silu(gate) * up_ref[...].astype(jnp.float32)).astype(jnp.bfloat16)

    pl.semaphore_wait(barrier, len(peers) + 2)

    def columns(row):
        return pl.ds(pl.multiple_of(row * width, LANES), width)

    my_rows = pl.ds(pl.multiple_of((c * n_row + r) * tok, tok), tok)
    own_copy = pltpu.make_async_copy(own.at[:, columns(r)], row_ref.at[my_rows], own_sem)
    swaps = []
    for i, peer in enumerate(peers):
        swaps.append(
            pltpu.make_async_remote_copy(
                src_ref=own.at[:, columns(peer)],
                dst_ref=row_ref.at[my_rows],
                send_sem=x_send.at[i],
                recv_sem=x_recv.at[i],
                device_id={"row": peer, "col": c},
                device_id_type=MESH,
            )
        )
    swaps[0].start()
    own_copy.start()
    swaps[1].start()
    swaps[2].start()
    for copy in hess_copies:
        copy.start()

    pair = 2 * tok
    pair_of = (lax.div(r, 2), 1 - lax.div(r, 2))

    def rows(source, g):
        return pl.ds(pl.multiple_of((source * n_row + 2 * pair_of[g]) * tok, pair), pair)

    def ring(d, s, g):
        piece = rows(at(place - (s - 1) if d == 0 else place + (s - 1)), g)
        return pltpu.make_async_remote_copy(
            src_ref=row_ref.at[piece],
            dst_ref=row_ref.at[piece],
            send_sem=ring_send.at[d, s - 1, g],
            recv_sem=ring_recv.at[d, s - 1, g],
            device_id={"row": r, "col": nexts[d]},
            device_id_type=MESH,
        )

    source_row = lax.div(c, 2)
    is_source = r == source_row
    is_sib = sib == source_row
    is_far = far == source_row
    is_last = far_sib == source_row
    panel = pl.ds(pl.multiple_of(y * half_width, LANES), half_width)

    def pieces(k):
        if k < 2:
            return c, k
        d, s, g = events[k - 2]
        return at(place - s if d == 0 else place + s), g

    def col_rows(k):
        source, g = pieces(k)
        x_source = lax.div(source_row, 2)
        p = x_source if g == 0 else 1 - x_source
        return pl.ds(pl.multiple_of((source * n_row + 2 * p) * tok, pair), pair)

    def col_copy(k, lane, target, src):
        return pltpu.make_async_remote_copy(
            src_ref=src,
            dst_ref=col_ref.at[col_rows(k)],
            send_sem=c_send.at[lane, k],
            recv_sem=c_recv.at[k],
            device_id={"row": target, "col": c},
            device_id_type=MESH,
        )

    def from_rows(k, lane, target):
        return col_copy(k, lane, target, row_ref.at[col_rows(k), panel])

    def forward(k):
        return col_copy(k, 0, sib, col_ref.at[col_rows(k)])

    def local(k):
        return pltpu.make_async_copy(
            row_ref.at[col_rows(k), panel], col_ref.at[col_rows(k)], c_local.at[k]
        )

    hops = n_col // 2
    events = [(d, s, g) for s in range(1, hops) for g in range(2) for d in range(2)]
    events += [(0, hops, 0), (1, hops, 1)]
    n_pieces = len(events) + 2

    def share(k):
        @pl.when(is_source)
        def _():
            from_rows(k, 1, far).start()
            from_rows(k, 0, sib).start()
            local(k).start()

    def pass_on(k):
        @pl.when(is_far)
        def _():
            forward(k).wait_recv()
            forward(k).start()

    swaps[0].wait_recv()
    own_copy.wait()
    for d in range(2):
        ring(d, 1, 0).start()
    share(0)
    swaps[1].wait_recv()
    swaps[2].wait_recv()
    for d in range(2):
        ring(d, 1, 1).start()
    share(1)

    for j, (d, s, g) in enumerate(events):
        ring(d, s, g).wait_recv()
        if (d, s + 1, g) in events:
            ring(d, s + 1, g).start()
        share(j + 2)
        if j + 2 >= LAG:
            pass_on(j + 2 - LAG)
    for k in range(n_pieces - LAG, n_pieces):
        pass_on(k)

    for copy in hess_copies:
        copy.wait()
    for copy in swaps:
        copy.wait_send()
    for event in events:
        ring(*event).wait_send()

    @pl.when(is_source)
    def _():
        for k in range(n_pieces):
            from_rows(k, 1, far).wait_send()
            from_rows(k, 0, sib).wait_send()
            local(k).wait()

    @pl.when(is_far)
    def _():
        for k in range(n_pieces):
            forward(k).wait_send()

    @pl.when(jnp.logical_or(is_sib, is_last))
    def _():
        for k in range(n_pieces):
            forward(k).wait_recv()


def gram_kernel(keep, gain, row_ref, col_ref, hess_ref, out_ref):
    tile = out_ref.shape[0]
    i = pl.program_id(0)
    lhs = row_ref[:, pl.ds(pl.multiple_of(i * tile, LANES), tile)]
    gram = lax.dot_general(
        lhs, col_ref[...], (((0,), (0,)), ((), ())), preferred_element_type=jnp.float32
    )
    old = hess_ref[pl.ds(pl.multiple_of(i * tile, LANES), tile), :]
    out_ref[...] = keep * old + gain * gram


def on_device(gate_act, up_act, running_hessian):
    n_row = lax.axis_size("row")
    n_col = lax.axis_size("col")
    tok_dev = gate_act.shape[0]
    height, col_width = running_hessian.shape
    if n_row != 4 or n_col != 2 * n_row or col_width % LANES or tok_dev % 8:
        return on_device_plain(gate_act, up_act, running_hessian)
    tokens_all = tok_dev * n_row * n_col
    total = 4.0 * tokens_all
    vmem = pl.BlockSpec(memory_space=pltpu.VMEM)
    hops = n_col // 2
    n_pieces = 2 * n_col
    dma = pltpu.SemaphoreType.DMA
    row_panel, col_panel, old = pl.pallas_call(
        functools.partial(gather_kernel, n_row, n_col),
        out_shape=(
            jax.ShapeDtypeStruct((tokens_all, height), jnp.bfloat16),
            jax.ShapeDtypeStruct((tokens_all, col_width), jnp.bfloat16),
            jax.ShapeDtypeStruct((height, col_width), jnp.float32),
        ),
        in_specs=[vmem, vmem, pl.BlockSpec(memory_space=pl.ANY)],
        out_specs=(vmem, vmem, vmem),
        scratch_shapes=[
            pltpu.VMEM(gate_act.shape, jnp.bfloat16),
            dma((HESS_PARTS,)),
            dma(()),
            dma((n_row - 1,)),
            dma((n_row - 1,)),
            dma((2, hops, 2)),
            dma((2, hops, 2)),
            dma((2, n_pieces)),
            dma((n_pieces,)),
            dma((n_pieces,)),
        ],
        compiler_params=pltpu.CompilerParams(
            collective_id=0, has_side_effects=True, vmem_limit_bytes=VMEM_A
        ),
        name="gather",
    )(gate_act, up_act, running_hessian)
    tile = 2 * LANES
    return pl.pallas_call(
        functools.partial(gram_kernel, 3.0 * tokens_all / total, 2.0 / total),
        out_shape=jax.ShapeDtypeStruct((height, col_width), jnp.float32),
        grid=(height // tile,),
        in_specs=[vmem, vmem, vmem],
        out_specs=pl.BlockSpec((tile, col_width), lambda i: (i, 0)),
        compiler_params=pltpu.CompilerParams(vmem_limit_bytes=VMEM_B),
        name="gram",
    )(row_panel, col_panel, old)


VMEM_A = 8 * 2**20
VMEM_B = 16 * 2**20


def solution(mesh):
    placed = (P(("row", "col"), None), P(("row", "col"), None), P("row", "col"))
    return jax.shard_map(
        on_device, mesh=mesh, in_specs=placed, out_specs=P("row", "col"), check_vma=False
    )
```

```python
import functools

import jax
import jax.numpy as jnp
from jax import lax
from jax.experimental import pallas as pl
from jax.experimental.pallas import tpu as pltpu
from jax.sharding import PartitionSpec as P

MESH = pl.DeviceIdType.MESH
LANES = 128
HESS_PARTS = 8
LAG = 2


def plain_inputs(gate_act, up_act):
    return (jax.nn.silu(gate_act.astype(jnp.float32)) * up_act.astype(jnp.float32)).astype(
        jnp.bfloat16
    )


def on_device_plain(gate_act, up_act, running_hessian):
    n_row = lax.axis_size("row")
    n_col = lax.axis_size("col")
    tok_dev = gate_act.shape[0]
    col_width = running_hessian.shape[1]
    inputs = plain_inputs(gate_act, up_act)
    col_part = lax.all_to_all(inputs, "col", split_axis=1, concat_axis=0, tiled=True)
    col_panel = lax.all_gather(col_part, "row", axis=0, tiled=True)
    col_ordered = (
        col_panel.reshape(n_row, n_col, tok_dev, col_width).swapaxes(0, 1).reshape(-1, col_width)
    )
    row_part = lax.all_to_all(inputs, "row", split_axis=1, concat_axis=0, tiled=True)
    gram = lax.dot_general(
        lax.all_gather(row_part, "col", axis=0, tiled=True),
        col_ordered,
        (((0,), (0,)), ((), ())),
        preferred_element_type=jnp.float32,
    )
    tokens_all = tok_dev * n_row * n_col
    total = 4.0 * tokens_all
    return 3.0 * tokens_all / total * running_hessian + 2.0 / total * gram


def other_core(r):
    return r + 1 - 2 * lax.rem(r, 2)


def gather_kernel(
    n_row, n_col, gate_hbm, up_hbm, hess_hbm, row_ref, col_ref, hess_ref, gate_ref, up_ref, own,
    in_sem, hess_sem, own_sem, x_send, x_recv, ring_send, ring_recv, c_send, c_recv, c_local,
):
    gate_copy = pltpu.make_async_copy(gate_hbm, gate_ref, in_sem.at[0])
    up_copy = pltpu.make_async_copy(up_hbm, up_ref, in_sem.at[1])
    gate_copy.start()
    up_copy.start()
    tok, width = gate_ref.shape[0], row_ref.shape[1]
    half_width = col_ref.shape[1]
    r, c = lax.axis_index("row"), lax.axis_index("col")
    sib = other_core(r)
    far = lax.rem(r + 2, n_row)
    far_sib = other_core(far)
    peers = (sib, far, far_sib)

    y = lax.rem(c, 2)
    place = (1 - y) * lax.div(c, 2) + y * (n_col - 1 - lax.div(c, 2))

    def at(p):
        p = lax.rem(p + 2 * n_col, n_col)
        back = lax.div(p, n_col // 2)
        return (1 - back) * 2 * p + back * (2 * (n_col - 1 - p) + 1)

    nexts = (at(place + 1), at(place - 1))

    hess_rows = hess_ref.shape[0] // HESS_PARTS
    hess_copies = []
    for i in range(HESS_PARTS):
        part = pl.ds(i * hess_rows, hess_rows)
        hess_copies.append(
            pltpu.make_async_copy(hess_hbm.at[part], hess_ref.at[part], hess_sem.at[i])
        )

    barrier = pltpu.get_barrier_semaphore()
    for peer in peers:
        pl.semaphore_signal(barrier, inc=1, device_id={"row": peer, "col": c}, device_id_type=MESH)
    for peer in nexts:
        pl.semaphore_signal(barrier, inc=1, device_id={"row": r, "col": peer}, device_id_type=MESH)

    gate_copy.wait()
    up_copy.wait()
    gate = gate_ref[...].astype(jnp.float32)
    own[...] = (jax.nn.silu(gate) * up_ref[...].astype(jnp.float32)).astype(jnp.bfloat16)

    pl.semaphore_wait(barrier, len(peers) + 2)

    def columns(row):
        return pl.ds(pl.multiple_of(row * width, LANES), width)

    my_rows = pl.ds(pl.multiple_of((c * n_row + r) * tok, tok), tok)
    own_copy = pltpu.make_async_copy(own.at[:, columns(r)], row_ref.at[my_rows], own_sem)
    swaps = []
    for i, peer in enumerate(peers):
        swaps.append(
            pltpu.make_async_remote_copy(
                src_ref=own.at[:, columns(peer)],
                dst_ref=row_ref.at[my_rows],
                send_sem=x_send.at[i],
                recv_sem=x_recv.at[i],
                device_id={"row": peer, "col": c},
                device_id_type=MESH,
            )
        )
    pair = 2 * tok
    pair_of = (lax.div(r, 2), 1 - lax.div(r, 2))

    def rows(source, g):
        return pl.ds(pl.multiple_of((source * n_row + 2 * pair_of[g]) * tok, pair), pair)

    hops = n_col // 2

    def to_next(d, s, g, src, dst):
        return pltpu.make_async_remote_copy(
            src_ref=src,
            dst_ref=dst,
            send_sem=ring_send.at[d, s - 1, g],
            recv_sem=ring_recv.at[d, s - 1, g],
            device_id={"row": r, "col": nexts[d]},
            device_id_type=MESH,
        )

    def ring(d, s, g):
        piece = row_ref.at[rows(at(place - (s - 1) if d == 0 else place + (s - 1)), g)]
        return to_next(d, s, g, piece, piece)

    def last_hop(d, g, second):
        y_next = lax.rem(nexts[d], 2)
        side = 1 - y_next if second else y_next
        piece = row_ref.at[
            rows(at(place - (hops - 1) if d == 0 else place + (hops - 1)), g),
            pl.ds(pl.multiple_of(side * half_width, LANES), half_width),
        ]
        return to_next(d, hops, 1 - g if second else g, piece, piece)

    def start_first(g, source, src=None):
        block = row_ref.at[pl.ds(pl.multiple_of((c * n_row + source) * tok, tok), tok)]
        for d in range(2):
            to_next(d, 1, g, block if src is None else src, block).start()

    source_row = lax.div(c, 2)
    is_source = r == source_row
    is_sib = sib == source_row
    is_far = far == source_row
    is_last = far_sib == source_row
    panel = pl.ds(pl.multiple_of(y * half_width, LANES), half_width)

    def pieces(k):
        if k < 2:
            return c, k
        d, s, g = events[k - 2]
        return at(place - s if d == 0 else place + s), g

    def col_rows(k):
        source, g = pieces(k)
        x_source = lax.div(source_row, 2)
        p = x_source if g == 0 else 1 - x_source
        return pl.ds(pl.multiple_of((source * n_row + 2 * p) * tok, pair), pair)

    def col_copy(k, lane, target, src):
        return pltpu.make_async_remote_copy(
            src_ref=src,
            dst_ref=col_ref.at[col_rows(k)],
            send_sem=c_send.at[lane, k],
            recv_sem=c_recv.at[k],
            device_id={"row": target, "col": c},
            device_id_type=MESH,
        )

    def from_rows(k, lane, target):
        return col_copy(k, lane, target, row_ref.at[col_rows(k), panel])

    def forward(k):
        return col_copy(k, 0, sib, col_ref.at[col_rows(k)])

    def local(k):
        return pltpu.make_async_copy(
            row_ref.at[col_rows(k), panel], col_ref.at[col_rows(k)], c_local.at[k]
        )

    events = [(d, s, g) for s in range(1, hops) for g in range(2) for d in range(2)]
    finals = [(0, hops, 0), (1, hops, 1)]
    events += finals
    n_pieces = len(events) + 2

    n_direct = len(finals)

    def direct(k):
        return k >= n_pieces - n_direct

    def straight(k):
        return from_rows(k, 2, far_sib)

    def share(k):
        @pl.when(is_source)
        def _():
            from_rows(k, 1, far).start()
            if direct(k):
                straight(k).start()
            from_rows(k, 0, sib).start()
            local(k).start()

    def pass_on(k):
        @pl.when(is_far)
        def _():
            forward(k).wait_recv()
            if not direct(k):
                forward(k).start()

    start_first(0, r, own.at[:, columns(r)])
    swaps[0].start()
    swaps[1].start()
    swaps[2].start()
    own_copy.start()
    for copy in hess_copies:
        copy.start()
    swaps[0].wait_recv()
    start_first(0, sib)
    own_copy.wait()
    share(0)
    swaps[1].wait_recv()
    start_first(1, far)
    swaps[2].wait_recv()
    start_first(1, far_sib)
    share(1)

    for j, (d, s, g) in enumerate(events):
        if s < hops:
            ring(d, s, g).wait_recv()
        else:
            last_hop(d, g, False).wait_recv()
        if (d, s + 1, g) in finals:
            last_hop(d, g, False).start()
            last_hop(d, g, True).start()
        elif (d, s + 1, g) in events:
            ring(d, s + 1, g).start()
        share(j + 2)
        if j + 2 >= LAG:
            pass_on(j + 2 - LAG)
    for k in range(n_pieces - LAG, n_pieces):
        pass_on(k)

    for copy in hess_copies:
        copy.wait()
    for copy in swaps:
        copy.wait_send()
    for d, s, g in events:
        if s < hops:
            ring(d, s, g).wait_send()
        else:
            last_hop(d, g, True).wait_recv()
            last_hop(d, g, False).wait_send()
            last_hop(d, g, True).wait_send()

    @pl.when(is_source)
    def _():
        for k in range(n_pieces):
            from_rows(k, 1, far).wait_send()
            from_rows(k, 0, sib).wait_send()
            local(k).wait()
            if direct(k):
                straight(k).wait_send()

    @pl.when(is_far)
    def _():
        for k in range(n_pieces):
            if not direct(k):
                forward(k).wait_send()

    @pl.when(jnp.logical_or(is_sib, is_last))
    def _():
        for k in range(n_pieces):
            forward(k).wait_recv()


def gram_kernel(keep, gain, row_ref, col_ref, hess_ref, out_ref):
    tile = out_ref.shape[0]
    i = pl.program_id(0)
    lhs = row_ref[:, pl.ds(pl.multiple_of(i * tile, LANES), tile)]
    gram = lax.dot_general(
        lhs, col_ref[...], (((0,), (0,)), ((), ())), preferred_element_type=jnp.float32
    )
    old = hess_ref[pl.ds(pl.multiple_of(i * tile, LANES), tile), :]
    out_ref[...] = keep * old + gain * gram


def on_device(gate_act, up_act, running_hessian):
    n_row = lax.axis_size("row")
    n_col = lax.axis_size("col")
    tok_dev = gate_act.shape[0]
    height, col_width = running_hessian.shape
    if n_row != 4 or n_col != 2 * n_row or col_width % LANES or tok_dev % 8:
        return on_device_plain(gate_act, up_act, running_hessian)
    tokens_all = tok_dev * n_row * n_col
    total = 4.0 * tokens_all
    in_hbm = functools.partial(pltpu.with_memory_space_constraint, memory_space=pltpu.HBM)
    vmem = pl.BlockSpec(memory_space=pltpu.VMEM)
    hops = n_col // 2
    n_pieces = 2 * n_col
    dma = pltpu.SemaphoreType.DMA
    row_panel, col_panel, old = pl.pallas_call(
        functools.partial(gather_kernel, n_row, n_col),
        out_shape=(
            jax.ShapeDtypeStruct((tokens_all, height), jnp.bfloat16),
            jax.ShapeDtypeStruct((tokens_all, col_width), jnp.bfloat16),
            jax.ShapeDtypeStruct((height, col_width), jnp.float32),
        ),
        in_specs=[pl.BlockSpec(memory_space=pltpu.HBM)] * 3,
        out_specs=(vmem, vmem, vmem),
        scratch_shapes=[
            pltpu.VMEM(gate_act.shape, jnp.bfloat16),
            pltpu.VMEM(gate_act.shape, jnp.bfloat16),
            pltpu.VMEM(gate_act.shape, jnp.bfloat16),
            dma((2,)),
            dma((HESS_PARTS,)),
            dma(()),
            dma((n_row - 1,)),
            dma((n_row - 1,)),
            dma((2, hops, 2)),
            dma((2, hops, 2)),
            dma((3, n_pieces)),
            dma((n_pieces,)),
            dma((n_pieces,)),
        ],
        compiler_params=pltpu.CompilerParams(
            collective_id=0, has_side_effects=True, vmem_limit_bytes=VMEM_A
        ),
        name="gather",
    )(in_hbm(gate_act), in_hbm(up_act), running_hessian)
    tile = height // 7 if height % (7 * LANES) == 0 else LANES
    return pl.pallas_call(
        functools.partial(gram_kernel, 3.0 * tokens_all / total, 2.0 / total),
        out_shape=jax.ShapeDtypeStruct((height, col_width), jnp.float32),
        grid=(height // tile,),
        in_specs=[vmem, vmem, vmem],
        out_specs=pl.BlockSpec((tile, col_width), lambda i: (i, 0)),
        compiler_params=pltpu.CompilerParams(vmem_limit_bytes=VMEM_B),
        name="gram",
    )(row_panel, col_panel, old)


VMEM_A = 8 * 2**20
VMEM_B = 24 * 2**20


def solution(mesh):
    placed = (P(("row", "col"), None), P(("row", "col"), None), P("row", "col"))
    return jax.shard_map(
        on_device, mesh=mesh, in_specs=placed, out_specs=P("row", "col"), check_vma=False
    )
```

```python
import functools

import jax
import jax.numpy as jnp
from jax import lax
from jax.experimental import pallas as pl
from jax.experimental.pallas import tpu as pltpu
from jax.sharding import PartitionSpec as P

MESH = pl.DeviceIdType.MESH
LANES = 128
HESS_PARTS = 8
LAG = 2


def plain_inputs(gate_act, up_act):
    return (jax.nn.silu(gate_act.astype(jnp.float32)) * up_act.astype(jnp.float32)).astype(
        jnp.bfloat16
    )


def on_device_plain(gate_act, up_act, running_hessian):
    n_row = lax.axis_size("row")
    n_col = lax.axis_size("col")
    tok_dev = gate_act.shape[0]
    col_width = running_hessian.shape[1]
    inputs = plain_inputs(gate_act, up_act)
    col_part = lax.all_to_all(inputs, "col", split_axis=1, concat_axis=0, tiled=True)
    col_panel = lax.all_gather(col_part, "row", axis=0, tiled=True)
    col_ordered = (
        col_panel.reshape(n_row, n_col, tok_dev, col_width).swapaxes(0, 1).reshape(-1, col_width)
    )
    row_part = lax.all_to_all(inputs, "row", split_axis=1, concat_axis=0, tiled=True)
    gram = lax.dot_general(
        lax.all_gather(row_part, "col", axis=0, tiled=True),
        col_ordered,
        (((0,), (0,)), ((), ())),
        preferred_element_type=jnp.float32,
    )
    tokens_all = tok_dev * n_row * n_col
    total = 4.0 * tokens_all
    return 3.0 * tokens_all / total * running_hessian + 2.0 / total * gram


def other_core(r):
    return r + 1 - 2 * lax.rem(r, 2)


def gather_kernel(
    n_row, n_col, gate_hbm, up_hbm, hess_hbm, row_ref, col_ref, hess_ref, gate_ref, up_ref, own,
    in_sem, hess_sem, own_sem, x_send, x_recv, ring_send, ring_recv, c_send, c_recv, c_local,
):
    gate_copy = pltpu.make_async_copy(gate_hbm, gate_ref, in_sem.at[0])
    up_copy = pltpu.make_async_copy(up_hbm, up_ref, in_sem.at[1])
    gate_copy.start()
    up_copy.start()
    tok, width = gate_ref.shape[0], row_ref.shape[1]
    half_width = col_ref.shape[1]
    r, c = lax.axis_index("row"), lax.axis_index("col")
    sib = other_core(r)
    far = lax.rem(r + 2, n_row)
    far_sib = other_core(far)
    peers = (sib, far, far_sib)

    y = lax.rem(c, 2)
    place = (1 - y) * lax.div(c, 2) + y * (n_col - 1 - lax.div(c, 2))

    def at(p):
        p = lax.rem(p + 2 * n_col, n_col)
        back = lax.div(p, n_col // 2)
        return (1 - back) * 2 * p + back * (2 * (n_col - 1 - p) + 1)

    nexts = (at(place + 1), at(place - 1))

    hess_rows = hess_ref.shape[0] // HESS_PARTS
    hess_copies = []
    for i in range(HESS_PARTS):
        part = pl.ds(i * hess_rows, hess_rows)
        hess_copies.append(
            pltpu.make_async_copy(hess_hbm.at[part], hess_ref.at[part], hess_sem.at[i])
        )

    barrier = pltpu.get_barrier_semaphore()
    for peer in peers:
        pl.semaphore_signal(barrier, inc=1, device_id={"row": peer, "col": c}, device_id_type=MESH)
    for peer in nexts:
        pl.semaphore_signal(barrier, inc=1, device_id={"row": r, "col": peer}, device_id_type=MESH)

    gate_copy.wait()
    up_copy.wait()
    gate = gate_ref[...].astype(jnp.float32)
    own[...] = (jax.nn.silu(gate) * up_ref[...].astype(jnp.float32)).astype(jnp.bfloat16)

    pl.semaphore_wait(barrier, len(peers) + 2)

    def columns(row):
        return pl.ds(pl.multiple_of(row * width, LANES), width)

    my_rows = pl.ds(pl.multiple_of((c * n_row + r) * tok, tok), tok)
    own_copy = pltpu.make_async_copy(own.at[:, columns(r)], row_ref.at[my_rows], own_sem)
    swaps = []
    for i, peer in enumerate(peers):
        swaps.append(
            pltpu.make_async_remote_copy(
                src_ref=own.at[:, columns(peer)],
                dst_ref=row_ref.at[my_rows],
                send_sem=x_send.at[i],
                recv_sem=x_recv.at[i],
                device_id={"row": peer, "col": c},
                device_id_type=MESH,
            )
        )
    pair = 2 * tok
    pair_of = (lax.div(r, 2), 1 - lax.div(r, 2))

    def rows(source, g):
        return pl.ds(pl.multiple_of((source * n_row + 2 * pair_of[g]) * tok, pair), pair)

    hops = n_col // 2

    def to_next(d, s, g, src, dst):
        return pltpu.make_async_remote_copy(
            src_ref=src,
            dst_ref=dst,
            send_sem=ring_send.at[d, s - 1, g],
            recv_sem=ring_recv.at[d, s - 1, g],
            device_id={"row": r, "col": nexts[d]},
            device_id_type=MESH,
        )

    def ring(d, s, g):
        piece = row_ref.at[rows(at(place - (s - 1) if d == 0 else place + (s - 1)), g)]
        return to_next(d, s, g, piece, piece)

    def last_hop(d, g, second):
        y_next = lax.rem(nexts[d], 2)
        side = 1 - y_next if second else y_next
        piece = row_ref.at[
            rows(at(place - (hops - 1) if d == 0 else place + (hops - 1)), g),
            pl.ds(pl.multiple_of(side * half_width, LANES), half_width),
        ]
        return to_next(d, hops, 1 - g if second else g, piece, piece)

    def start_first(g, source, src=None):
        block = row_ref.at[pl.ds(pl.multiple_of((c * n_row + source) * tok, tok), tok)]
        for d in range(2):
            to_next(d, 1, g, block if src is None else src, block).start()

    source_row = lax.div(c, 2)
    is_source = r == source_row
    is_sib = sib == source_row
    is_far = far == source_row
    is_last = far_sib == source_row
    panel = pl.ds(pl.multiple_of(y * half_width, LANES), half_width)

    def pieces(k):
        if k < 2:
            return c, k
        d, s, g = events[k - 2]
        return at(place - s if d == 0 else place + s), g

    def col_rows(k):
        source, g = pieces(k)
        x_source = lax.div(source_row, 2)
        p = x_source if g == 0 else 1 - x_source
        return pl.ds(pl.multiple_of((source * n_row + 2 * p) * tok, pair), pair)

    def col_copy(k, lane, target, src):
        return pltpu.make_async_remote_copy(
            src_ref=src,
            dst_ref=col_ref.at[col_rows(k)],
            send_sem=c_send.at[lane, k],
            recv_sem=c_recv.at[k],
            device_id={"row": target, "col": c},
            device_id_type=MESH,
        )

    def from_rows(k, lane, target):
        return col_copy(k, lane, target, row_ref.at[col_rows(k), panel])

    def forward(k):
        return col_copy(k, 0, sib, col_ref.at[col_rows(k)])

    def local(k):
        return pltpu.make_async_copy(
            row_ref.at[col_rows(k), panel], col_ref.at[col_rows(k)], c_local.at[k]
        )

    events = [(d, s, g) for s in range(1, hops) for g in range(2) for d in range(2)]
    finals = [(0, hops, 0), (1, hops, 1)]
    events += finals
    n_pieces = len(events) + 2

    n_direct = len(finals)

    def direct(k):
        return k >= n_pieces - n_direct

    def straight(k):
        return from_rows(k, 2, far_sib)

    def share(k):
        @pl.when(is_source)
        def _():
            from_rows(k, 1, far).start()
            if direct(k):
                straight(k).start()
            from_rows(k, 0, sib).start()
            local(k).start()

    def pass_on(k):
        @pl.when(is_far)
        def _():
            forward(k).wait_recv()
            if not direct(k):
                forward(k).start()

    start_first(0, r, own.at[:, columns(r)])
    swaps[0].start()
    swaps[1].start()
    swaps[2].start()
    own_copy.start()
    for copy in hess_copies:
        copy.start()
    swaps[0].wait_recv()
    start_first(0, sib)
    own_copy.wait()
    share(0)
    swaps[1].wait_recv()
    start_first(1, far)
    swaps[2].wait_recv()
    start_first(1, far_sib)
    share(1)

    for j, (d, s, g) in enumerate(events):
        if s < hops:
            ring(d, s, g).wait_recv()
        else:
            last_hop(d, g, False).wait_recv()
        if (d, s + 1, g) in finals:
            last_hop(d, g, False).start()
            last_hop(d, g, True).start()
        elif (d, s + 1, g) in events:
            ring(d, s + 1, g).start()
        share(j + 2)
        if j + 2 >= LAG:
            pass_on(j + 2 - LAG)
    for k in range(n_pieces - LAG, n_pieces):
        pass_on(k)

    for copy in hess_copies:
        copy.wait()
    for copy in swaps:
        copy.wait_send()
    for d, s, g in events:
        if s < hops:
            ring(d, s, g).wait_send()
        else:
            last_hop(d, g, True).wait_recv()
            last_hop(d, g, False).wait_send()
            last_hop(d, g, True).wait_send()

    @pl.when(is_source)
    def _():
        for k in range(n_pieces):
            from_rows(k, 1, far).wait_send()
            from_rows(k, 0, sib).wait_send()
            local(k).wait()
            if direct(k):
                straight(k).wait_send()

    @pl.when(is_far)
    def _():
        for k in range(n_pieces):
            if not direct(k):
                forward(k).wait_send()

    @pl.when(jnp.logical_or(is_sib, is_last))
    def _():
        for k in range(n_pieces):
            forward(k).wait_recv()


def gram_kernel(keep, gain, strips, row_ref, col_ref, hess_ref, out_hbm, tiles, sems):
    tile = tiles.shape[1]
    i, n = pl.program_id(0), pl.num_programs(0)
    slot = lax.rem(i, 2)

    def copies(at_slot, at_tile):
        rows = pl.ds(pl.multiple_of(at_tile * tile, LANES), tile)
        return [
            pltpu.make_async_copy(
                tiles.at[at_slot, :, pl.ds(start, size)],
                out_hbm.at[rows, pl.ds(start, size)],
                sems.at[at_slot, k],
            )
            for k, (start, size) in enumerate(strips)
        ]

    @pl.when(i >= 2)
    def _():
        for copy in copies(slot, i - 2):
            copy.wait()

    rows = pl.ds(pl.multiple_of(i * tile, LANES), tile)
    out = copies(slot, i)
    for k, (start, size) in enumerate(strips):
        strip = slice(start, start + size)
        gram = lax.dot_general(
            row_ref[:, rows],
            col_ref[:, strip],
            (((0,), (0,)), ((), ())),
            preferred_element_type=jnp.float32,
        )
        tiles[slot, :, strip] = keep * hess_ref[rows, strip] + gain * gram
        out[k].start()

    @pl.when(i == n - 1)
    def _():
        for copy in copies(1 - slot, i - 1) + out:
            copy.wait()


def column_strips(width, count):
    blocks = width // LANES
    edges = [LANES * (blocks * k // count) for k in range(count + 1)]
    return [(a, b - a) for a, b in zip(edges, edges[1:])]


def on_device(gate_act, up_act, running_hessian):
    n_row = lax.axis_size("row")
    n_col = lax.axis_size("col")
    tok_dev = gate_act.shape[0]
    height, col_width = running_hessian.shape
    if n_row != 4 or n_col != 2 * n_row or col_width % LANES or tok_dev % 8:
        return on_device_plain(gate_act, up_act, running_hessian)
    tokens_all = tok_dev * n_row * n_col
    total = 4.0 * tokens_all
    in_hbm = functools.partial(pltpu.with_memory_space_constraint, memory_space=pltpu.HBM)
    vmem = pl.BlockSpec(memory_space=pltpu.VMEM)
    hops = n_col // 2
    n_pieces = 2 * n_col
    dma = pltpu.SemaphoreType.DMA
    row_panel, col_panel, old = pl.pallas_call(
        functools.partial(gather_kernel, n_row, n_col),
        out_shape=(
            jax.ShapeDtypeStruct((tokens_all, height), jnp.bfloat16),
            jax.ShapeDtypeStruct((tokens_all, col_width), jnp.bfloat16),
            jax.ShapeDtypeStruct((height, col_width), jnp.float32),
        ),
        in_specs=[pl.BlockSpec(memory_space=pltpu.HBM)] * 3,
        out_specs=(vmem, vmem, vmem),
        scratch_shapes=[
            pltpu.VMEM(gate_act.shape, jnp.bfloat16),
            pltpu.VMEM(gate_act.shape, jnp.bfloat16),
            pltpu.VMEM(gate_act.shape, jnp.bfloat16),
            dma((2,)),
            dma((HESS_PARTS,)),
            dma(()),
            dma((n_row - 1,)),
            dma((n_row - 1,)),
            dma((2, hops, 2)),
            dma((2, hops, 2)),
            dma((3, n_pieces)),
            dma((n_pieces,)),
            dma((n_pieces,)),
        ],
        compiler_params=pltpu.CompilerParams(
            collective_id=0, has_side_effects=True, vmem_limit_bytes=VMEM_A
        ),
        name="gather",
    )(in_hbm(gate_act), in_hbm(up_act), running_hessian)
    tile = height // 7 if height % (7 * LANES) == 0 else LANES
    strips = column_strips(col_width, STRIPS)
    return pl.pallas_call(
        functools.partial(gram_kernel, 3.0 * tokens_all / total, 2.0 / total, strips),
        out_shape=jax.ShapeDtypeStruct((height, col_width), jnp.float32),
        grid=(height // tile,),
        in_specs=[vmem, vmem, vmem],
        out_specs=pl.BlockSpec(memory_space=pltpu.HBM),
        scratch_shapes=[pltpu.VMEM((2, tile, col_width), jnp.float32), dma((2, len(strips)))],
        compiler_params=pltpu.CompilerParams(vmem_limit_bytes=VMEM_B),
        name="gram",
    )(row_panel, col_panel, old)


STRIPS = 7
VMEM_A = 8 * 2**20
VMEM_B = 24 * 2**20


def solution(mesh):
    placed = (P(("row", "col"), None), P(("row", "col"), None), P("row", "col"))
    return jax.shard_map(
        on_device, mesh=mesh, in_specs=placed, out_specs=P("row", "col"), check_vma=False
    )
```
